256 devices in a mesh: layer: 8 (over y_lo, x), feat: 32 (over z, y_hi, core).
Axes of the slice: x: 4, y: 4 (y_hi: 2, y_lo: 2; y = y_hi * 2 + y_lo), z: 8, core: 2. Of those that a mesh axis runs over, the one named last changes fastest.
Arguments:
- inputs: bfloat16 [8, 128, 2304], P('layer'), may hold values from -6 to 6
- targets: bfloat16 [8, 128, 2304], P('layer', None, 'feat'), may hold values from -6 to 6
- w_enc: bfloat16 [8, 2304, 2048], P('layer', None, 'feat'), may hold values from -0.125 to 0.125
- b_enc: float32 [8, 2048], P('layer', 'feat'), may hold values from -3 to 3
- w_dec: bfloat16 [8, 8, 2048, 2304], P('layer', None, 'feat'), may hold values from -0.046875 to 0.046875
Outputs:
- grad_enc: bfloat16 [8, 2304, 2048], P('layer', None, 'feat')
- grad_dec: bfloat16 [8, 8, 2048, 2304], P('layer', None, 'feat')
- grad_benc: float32 [8, 2048], P('layer', 'feat')
The draws below stay inside these ranges and needn't reach their ends.
All inputs are finite; a program needn't handle non-finite values.
Results may differ from the reference program's by a relative error of at most 0.0085.
Values may be sent and summed in bfloat16 or wider, within the bound.
A program may use at most 64 MiB of HBM per device.

```python
import jax
import jax.numpy as jnp
from jax import lax

D = 2304
F = 2048
TOK = 128
LAYERS = 8


def block_levels(stream_key, shape, split, smallest, top_value):
    level = 1.0
    for axis_at, shards_of in split:
        steps = jax.random.uniform(jax.random.fold_in(jax.random.fold_in(stream_key, 6), axis_at), (shards_of,), jnp.float32, smallest / len(split), top_value / len(split))
        level = level * jnp.repeat(jnp.exp(steps), shape[axis_at] // shards_of).reshape((-1,) + (1,) * (len(shape) - 1 - axis_at))
    return level


def bell_draw(key, shape, deviation, reach, shards=(), dtype=jnp.bfloat16):
    array = jax.random.normal(key, shape, jnp.float32) * deviation
    if len(shards) > 0:
        array = block_levels(key, shape, shards, -0.22, 0.18) * array
    return jnp.clip(array, min=-reach, max=reach).astype(dtype)


def setup_inputs(seed: int = 0) -> dict:
    keys = jax.random.split(jax.random.key(seed), 6)
    return {
        "inputs": bell_draw(keys[0], (LAYERS, TOK, D), 1.0, 6.0, ((0, 8),)),
        "targets": bell_draw(keys[1], (LAYERS, TOK, D), 1.0, 6.0, ((0, 8), (2, 32))),
        "w_enc": bell_draw(keys[2], (LAYERS, D, F), D ** -0.5, 0.125, ((0, 8), (2, 32))),
        "b_enc": bell_draw(keys[3], (LAYERS, F), 0.5, 3.0, ((0, 8), (1, 32)), jnp.float32),
        "w_dec": bell_draw(keys[4], (LAYERS, LAYERS, F, D), (F * LAYERS) ** -0.5, 0.046875, ((0, 8), (2, 32))),
    }


def reference(inputs, targets, w_enc, b_enc, w_dec):
    grad_scale = TOK ** -0.5
    layer_count = w_dec.shape[0]
    pre_act = jnp.einsum('ltd,ldf->ltf', inputs.astype(jnp.float32), w_enc.astype(jnp.float32)) + b_enc[:, None, :]
    active = jax.nn.relu(pre_act).astype(jnp.bfloat16)
    layer_ids = jnp.arange(layer_count)

    def recon_of(target_id):
        flag_rows = (layer_ids <= target_id).astype(jnp.float32)
        masked = active.astype(jnp.float32) * flag_rows[:, None, None]
        return jnp.einsum('ltf,lfd->td', masked, w_dec[:, target_id].astype(jnp.float32))

    rebuilt = lax.map(recon_of, layer_ids)
    errors = (rebuilt - targets.astype(jnp.float32)).astype(jnp.bfloat16)

    def source(source_id):
        flag_rows = (layer_ids >= source_id).astype(jnp.float32)
        masked = errors.astype(jnp.float32) * flag_rows[:, None, None]
        weights = w_dec[source_id].astype(jnp.float32)
        act_grad = grad_scale * jnp.einsum('mtd,mfd->tf', masked, weights)
        dec_grad = (grad_scale * jnp.einsum('tf,mtd->mfd', active[source_id].astype(jnp.float32), masked)).astype(jnp.bfloat16)
        return act_grad, dec_grad

    act_grad, grad_dec = lax.map(source, layer_ids)
    pre_grad = jnp.where(pre_act > 0, act_grad, 0.0).astype(jnp.bfloat16)
    grad_enc = jnp.einsum('ltd,ltf->ldf', inputs.astype(jnp.float32), pre_grad.astype(jnp.float32)).astype(jnp.bfloat16)
    grad_benc = jnp.sum(pre_grad.astype(jnp.float32), axis=1)
    return grad_enc, grad_dec, grad_benc
```

```python
import functools

import jax
import jax.numpy as jnp
from jax import lax
from jax.experimental import pallas as pl
from jax.experimental.pallas import tpu as pltpu
from jax.sharding import PartitionSpec as P

MESH = pl.DeviceIdType.MESH
F32 = jnp.float32
BF16 = jnp.bfloat16

NX = 4
NZ = 8
NT = (((1,), (1,)), ((), ()))


def kernel(
    scale,
    inputs_ref, targets_ref, wenc_ref, benc_ref, wdec_ref,
    genc_ref, gdec_ref, gb_ref,
    x_in, w_en, b_en, t_in, w_all, act_t, a_mat, pre_s, part, y_out, y_in,
    zp_out, zm_out, zp_in, zm_in, x_out, x_sum, x_rec, err, grads, zeros, acc, acc_in, ge_out, gb_out,
    load_sem, zero_sem, store_sem, fin_sem,
    w_s, w_r, t_s, t_r, a_s, a_r, c_s, c_r, g_s, g_r,
    y_s, y_r, zp_s, zp_r, zm_s, zm_r, x_s, x_r, e_s, e_r, ep_s, ep_r, em_s, em_r, b_s, b_r,
):
    lay = lax.axis_index("layer")
    ft = lax.axis_index("feat")
    y_lo = lay // NX
    x = lay % NX
    z = ft // 4
    y_hi = (ft // 2) % 2
    c = ft % 2
    half = w_all.shape[2]
    slab = wdec_ref.shape[1]

    def feat_of(zz, hh):
        return zz * 4 + hh * 2 + c

    partner = (lay, ft + 1 - 2 * c)
    z_up = (lay, feat_of((z + 1) % NZ, y_hi))
    z_dn = (lay, feat_of((z + NZ - 1) % NZ, y_hi))
    other_lay = (1 - y_lo) * NX + x
    my_cols = pl.ds(pl.multiple_of(c * half, 128), half)
    their_cols = pl.ds(pl.multiple_of((1 - c) * half, 128), half)

    def remote(src, dst, s, r, dev):
        return pltpu.make_async_remote_copy(
            src_ref=src, dst_ref=dst, send_sem=s, recv_sem=r, device_id=dev, device_id_type=MESH
        )

    ld_w = [
        pltpu.make_async_copy(wenc_ref, w_en, load_sem.at[0]),
        pltpu.make_async_copy(inputs_ref, x_in, load_sem.at[1]),
        pltpu.make_async_copy(benc_ref, b_en, load_sem.at[2]),
        pltpu.make_async_copy(targets_ref, t_in.at[0], load_sem.at[3]),
    ]
    for d in ld_w:
        d.start()

    def own_w(m):
        return pltpu.make_async_copy(
            wdec_ref.at[m, :, my_cols], w_all.at[m, pl.ds(0, slab), :], load_sem.at[4 + m]
        )

    def load_body(m, _):
        own_w(m).start()
        return 0

    lax.fori_loop(lay, 8, load_body, 0)

    barrier = pltpu.get_barrier_semaphore()

    def greet(dev):
        pl.semaphore_signal(barrier, inc=1, device_id=dev, device_id_type=MESH)

    greet(partner)
    greet(z_up)
    greet(z_dn)
    greet((other_lay, feat_of(z, y_hi)))
    greet((other_lay, feat_of(z, 1 - y_hi)))
    for k in range(1, NX):
        mate = y_lo * NX + (x + k) % NX
        greet((mate, feat_of(z, y_hi)))
        greet((mate, feat_of(z, 1 - y_hi)))
    greet((lay, feat_of(z, 1 - y_hi)))
    zeros[...] = jnp.zeros_like(zeros)
    pl.semaphore_wait(barrier, 12)

    def swap_w(m):
        return remote(
            wdec_ref.at[m, :, their_cols], w_all.at[m, pl.ds(slab, slab), :], w_s.at[m], w_r.at[m], partner
        )

    swap_t = remote(targets_ref, t_in.at[1], t_s, t_r, partner)
    swap_t.start()

    def swap_body(k, _):
        swap_w(7 - k).start()
        return 0

    lax.fori_loop(0, 8 - lay, swap_body, 0)

    def zero_copy(m):
        return pltpu.make_async_copy(zeros, gdec_ref.at[m], zero_sem.at[m])

    def zero_body(m, _):
        zero_copy(m).start()
        return 0

    lax.fori_loop(0, lay, zero_body, 0)

    row = lax.broadcasted_iota(jnp.int32, (slab, slab), 0)
    col = lax.broadcasted_iota(jnp.int32, (slab, slab), 1)
    ld_w[2].wait()
    bias = jnp.sum(jnp.where(row == col, b_en[...], 0.0), axis=1, keepdims=True)
    ld_w[0].wait()
    ld_w[1].wait()
    pre = lax.dot_general(w_en[...], x_in[...], NT, preferred_element_type=F32) + bias
    pre_s[...] = pre
    act_t[pl.ds(0, slab), :] = jnp.maximum(pre, 0.0).astype(BF16)
    swap_a = remote(act_t.at[pl.ds(0, slab), :], act_t.at[pl.ds(slab, slab), :], a_s, a_r, partner)
    swap_a.start()
    ld_w[3].wait()
    swap_t.wait_recv()
    swap_a.wait_recv()
    a_mat[...] = act_t[...].T

    chunk = 384

    def wait_w(m):
        own_w(m).wait()
        swap_w(m).wait_recv()

    def y_copy(j, tb):
        dev = (other_lay, feat_of(z, (y_hi + tb) % 2))
        return remote(y_out.at[j, tb], y_in.at[j, tb], y_s.at[j, tb], y_r.at[j, tb], dev)

    order = (4, NZ - 3, 3, NZ - 2, 2, NZ - 1, 1, 0)

    @pl.when(y_lo == 0)
    def _():
        def up_body(j, _):
            m = NX + j
            wait_w(m)
            for n in range(0, half, chunk):
                p = jnp.dot(a_mat[...], w_all[m, :, pl.ds(n, chunk)], preferred_element_type=F32)
                y_out[j, :, :, pl.ds(n, chunk)] = p.astype(BF16).reshape(NZ, 16, chunk)
            return 0

        lax.fori_loop(0, NX, up_body, 0)
        for off in order:
            tb = (z + off) % NZ

            def send_body(j, _):
                y_copy(j, tb).start()
                return 0

            lax.fori_loop(0, NX, send_body, 0)

    lo = jnp.where(y_lo == 1, 0, x)
    n_act = NX - lo

    def row_body(j, _):
        m = y_lo * NX + j

        @pl.when(m >= lay)
        def _():
            wait_w(m)
            for n in range(0, half, chunk):
                p = jnp.dot(a_mat[...], w_all[m, :, pl.ds(n, chunk)], preferred_element_type=F32)
                part[j, :, :, pl.ds(n, chunk)] = p.reshape(NZ, 16, chunk)

        @pl.when(m < lay)
        def _():
            part[j] = jnp.zeros(part.shape[1:], F32)

        return 0

    lax.fori_loop(lo, NX, row_body, 0)

    @pl.when(z // 4 == c)
    def _():
        width = t_in.shape[1]
        for k in range(2):
            core = c if k == 0 else 1 - c
            start = width * (2 * ((2 * z + y_hi) % NZ) + core)
            tt = t_in[k].astype(F32).T.astype(BF16)
            for n in range(0, half, chunk):
                jj = lax.broadcasted_iota(jnp.int32, (width, chunk), 0) + start
                nn = lax.broadcasted_iota(jnp.int32, (width, chunk), 1) + n
                sel = jnp.where(jj == nn, -1.0, 0.0).astype(BF16)
                t_full = jnp.dot(tt, sel, preferred_element_type=F32)
                part[x, :, :, pl.ds(n, chunk)] = part[x, :, :, pl.ds(n, chunk)] + t_full.reshape(
                    NZ, 16, chunk
                )

    def absorb(j, tb):
        @pl.when(y_lo == 1)
        def _():
            y_copy(j, tb).wait_recv()
            part[j, tb] = part[j, tb] + y_in[j, tb].astype(F32)

    def rs_up(s, j):
        return remote(zp_out.at[s, j], zp_in.at[s, j], zp_s.at[s, j], zp_r.at[s, j], z_up)

    def rs_dn(s, j):
        return remote(zm_out.at[s, j], zm_in.at[s, j], zm_s.at[s, j], zm_r.at[s, j], z_dn)

    for s in range(4):
        t_up = (z + 4 - s) % NZ
        t_dn = (z + NZ - 3 + s) % NZ

        def rs_body(j, _):
            absorb(j, t_up)
            v = part[j, t_up]
            if s > 0:
                rs_up(s - 1, j).wait_recv()
                v = v + zp_in[s - 1, j].astype(F32)
            zp_out[s, j] = v.astype(BF16)
            rs_up(s, j).start()
            if s < 3:
                absorb(j, t_dn)
                w = part[j, t_dn]
                if s > 0:
                    rs_dn(s - 1, j).wait_recv()
                    w = w + zm_in[s - 1, j].astype(F32)
                zm_out[s, j] = w.astype(BF16)
                rs_dn(s, j).start()
            return 0

        lax.fori_loop(lo, NX, rs_body, 0)

    def x_same(j):
        return remote(
            x_out.at[j], x_rec.at[x], x_s.at[j], x_r.at[x], (y_lo * NX + j, feat_of(z, y_hi))
        )

    def x_twin(j):
        return remote(
            x_out.at[j], x_rec.at[NX + x], x_s.at[NX + j], x_r.at[NX + x], (y_lo * NX + j, feat_of(z, 1 - y_hi))
        )

    def x_wait(slot):
        remote(x_out.at[0], x_rec.at[slot], x_s.at[0], x_r.at[slot], partner).wait_recv()

    def x_body(j, _):
        absorb(j, z)
        rs_dn(2, j).wait_recv()
        rs_up(3, j).wait_recv()
        v = part[j, z] + zm_in[2, j].astype(F32) + zp_in[3, j].astype(F32)
        x_out[j] = v.astype(BF16)
        x_twin(j).start()

        @pl.when(j != x)
        def _():
            x_same(j).start()

        @pl.when(j == x)
        def _():
            x_sum[...] = v

        return 0

    lax.fori_loop(lo, NX, x_body, 0)

    n_src = jnp.where(y_lo == 1, NX, x + 1)

    def sum_body(xx, _):
        @pl.when(xx != x)
        def _():
            x_wait(xx)
            x_sum[...] = x_sum[...] + x_rec[xx].astype(F32)

        x_wait(NX + xx)
        x_sum[...] = x_sum[...] + x_rec[NX + xx].astype(F32)
        return 0

    lax.fori_loop(0, n_src, sum_body, 0)
    err[lay, z] = x_sum[...].astype(BF16)

    def e_send(xx):
        return remote(
            err.at[lay, z], err.at[lay, z], e_s.at[xx], e_r.at[x], (y_lo * NX + xx, feat_of(z, y_hi))
        )

    def e_wait(j):
        remote(err.at[lay, z], err.at[y_lo * NX + j, z], e_s.at[0], e_r.at[j], partner).wait_recv()

    n_dst = jnp.where(y_lo == 1, NX, x)

    def e_body(xx, _):
        @pl.when(xx != x)
        def _():
            e_send(xx).start()

        return 0

    lax.fori_loop(0, n_dst, e_body, 0)

    def ag_up(s, j, tb):
        piece = err.at[y_lo * NX + j, tb]
        return remote(piece, piece, ep_s.at[s, j], ep_r.at[s, j], z_up)

    def ag_dn(s, j, tb):
        piece = err.at[y_lo * NX + j, tb]
        return remote(piece, piece, em_s.at[s, j], em_r.at[s, j], z_dn)

    def back(j, tb):
        piece = err.at[NX + j, tb]
        return remote(
            piece, piece, b_s.at[j, tb], b_r.at[j, tb], (other_lay, feat_of(z, (y_hi + tb) % 2))
        )

    def forward_back(j, tb):
        @pl.when(y_lo == 1)
        def _():
            back(j, tb).start()

    def gdec_own(m):
        return pltpu.make_async_copy(
            grads.at[m, pl.ds(0, slab), :], gdec_ref.at[m, :, my_cols], store_sem.at[m]
        )

    def gdec_peer(m):
        return remote(
            grads.at[m, pl.ds(slab, slab), :], gdec_ref.at[m, :, my_cols], g_s.at[m], g_r.at[m], partner
        )

    def gdec_wait(m):
        remote(
            grads.at[m, pl.ds(slab, slab), :], gdec_ref.at[m, :, their_cols], g_s.at[m], g_r.at[m], partner
        ).wait_recv()

    acc[...] = jnp.zeros_like(acc)

    def backward(m):
        for n in range(0, half, chunk):
            e = err[m, :, :, pl.ds(n, chunk)].reshape(NZ * 16, chunk)
            g = jnp.dot(act_t[...], e, preferred_element_type=F32) * scale
            grads[m, :, pl.ds(n, chunk)] = g.astype(BF16)
        gdec_peer(m).start()
        gdec_own(m).start()
        e = err[m].reshape(NZ * 16, half)
        acc[...] = acc[...] + lax.dot_general(w_all[m], e, NT, preferred_element_type=F32)

    for s in range(5):
        t_up = (z + NZ - s) % NZ
        t_dn = (z + s) % NZ

        def ag_body(k, _):
            j = (x + k) % NX
            if s == 0:

                @pl.when(k > 0)
                def _():
                    e_wait(j)

                ag_up(0, j, z).start()
                ag_dn(0, j, z).start()
                forward_back(j, z)
            else:
                ag_up(s - 1, j, t_up).wait_recv()
                if s < 4:
                    ag_up(s, j, t_up).start()
                forward_back(j, t_up)
                if s < 4:
                    ag_dn(s - 1, j, t_dn).wait_recv()
                    if s < 3:
                        ag_dn(s, j, t_dn).start()
                    forward_back(j, t_dn)
            if s == 4:

                @pl.when(j >= x)
                def _():
                    backward(y_lo * NX + j)

            return 0

        lax.fori_loop(0, n_act, ag_body, 0)

    @pl.when(y_lo == 0)
    def _():
        def up_back(j, _):
            def wait_body(tb, _):
                back(j, tb).wait_recv()
                return 0

            lax.fori_loop(0, NZ, wait_body, 0)
            backward(NX + j)
            return 0

        lax.fori_loop(0, NX, up_back, 0)

    swap_c = remote(acc.at[pl.ds(slab, slab), :], acc_in, c_s, c_r, partner)
    swap_c.start()
    swap_c.wait_recv()
    act_grad = (acc[pl.ds(0, slab), :] + acc_in[...]) * scale
    pre_grad = jnp.where(pre_s[...] > 0.0, act_grad, 0.0).astype(BF16)
    ge_out[...] = jnp.dot(pre_grad, x_in[...], preferred_element_type=F32).astype(BF16)
    total = jnp.sum(pre_grad.astype(F32), axis=1, keepdims=True)
    gb_out[...] = jnp.sum(jnp.where(row == col, total, 0.0), axis=0, keepdims=True)
    st_e = pltpu.make_async_copy(ge_out, genc_ref, fin_sem.at[0])
    st_b = pltpu.make_async_copy(gb_out, gb_ref, fin_sem.at[1])
    st_e.start()
    st_b.start()

    swap_t.wait_send()
    swap_a.wait_send()
    swap_c.wait_send()

    def own_done(m, _):
        swap_w(m).wait_send()
        gdec_own(m).wait()
        gdec_peer(m).wait_send()
        gdec_wait(m)
        return 0

    lax.fori_loop(lay, 8, own_done, 0)

    def zero_done(m, _):
        zero_copy(m).wait()
        return 0

    lax.fori_loop(0, lay, zero_done, 0)

    def chain_done(j, _):
        for s in range(4):
            rs_up(s, j).wait_send()
            ag_up(s, j, z).wait_send()
        for s in range(3):
            rs_dn(s, j).wait_send()
            ag_dn(s, j, z).wait_send()
        x_twin(j).wait_send()

        @pl.when(j != x)
        def _():
            x_same(j).wait_send()

        return 0

    lax.fori_loop(lo, NX, chain_done, 0)

    def e_done(xx, _):
        @pl.when(xx != x)
        def _():
            e_send(xx).wait_send()

        return 0

    lax.fori_loop(0, n_dst, e_done, 0)

    def y_done(i, _):
        @pl.when(y_lo == 0)
        def _():
            y_copy(i // NZ, i % NZ).wait_send()

        @pl.when(y_lo == 1)
        def _():
            back(i // NZ, i % NZ).wait_send()

        return 0

    lax.fori_loop(0, NX * NZ, y_done, 0)
    st_e.wait()
    st_b.wait()


def shards(inputs, targets, w_enc, b_enc, w_dec):
    tok, width = inputs.shape[1], inputs.shape[2]
    n_lay, slab = w_dec.shape[1], w_dec.shape[2]
    half = width // 2
    tcols = targets.shape[2]
    dma = pltpu.SemaphoreType.DMA
    vm = pltpu.VMEM
    any_spec = pl.BlockSpec(memory_space=pl.ANY)
    piece = (16, half)
    outs = pl.pallas_call(
        functools.partial(kernel, tok ** (-0.5)),
        out_shape=(
            jax.ShapeDtypeStruct((slab, width), BF16),
            jax.ShapeDtypeStruct((n_lay, slab, width), BF16),
            jax.ShapeDtypeStruct((1, slab), F32),
        ),
        in_specs=[any_spec] * 5,
        out_specs=(any_spec,) * 3,
        scratch_shapes=[
            vm((tok, width), BF16),
            vm((slab, width), BF16),
            vm((1, slab), F32),
            vm((2, tcols, tok), BF16),
            vm((n_lay, 2 * slab, half), BF16),
            vm((2 * slab, tok), BF16),
            vm((tok, 2 * slab), BF16),
            vm((slab, tok), F32),
            vm((NX, NZ) + piece, F32),
            vm((NX, NZ) + piece, BF16),
            vm((NX, NZ) + piece, BF16),
            vm((4, NX) + piece, BF16),
            vm((3, NX) + piece, BF16),
            vm((4, NX) + piece, BF16),
            vm((3, NX) + piece, BF16),
            vm((NX,) + piece, BF16),
            vm(piece, F32),
            vm((2 * NX,) + piece, BF16),
            vm((n_lay, NZ) + piece, BF16),
            vm((n_lay, 2 * slab, half), BF16),
            vm((slab, width), BF16),
            vm((2 * slab, tok), F32),
            vm((slab, tok), F32),
            vm((slab, width), BF16),
            vm((1, slab), F32),
            dma((4 + n_lay,)),
            dma((n_lay,)),
            dma((n_lay,)),
            dma((2,)),
            dma((n_lay,)), dma((n_lay,)),
            dma, dma,
            dma, dma,
            dma, dma,
            dma((n_lay,)), dma((n_lay,)),
            dma((NX, NZ)), dma((NX, NZ)),
            dma((4, NX)), dma((4, NX)),
            dma((3, NX)), dma((3, NX)),
            dma((2 * NX,)), dma((2 * NX,)),
            dma((NX,)), dma((NX,)),
            dma((4, NX)), dma((4, NX)),
            dma((3, NX)), dma((3, NX)),
            dma((NX, NZ)), dma((NX, NZ)),
        ],
        compiler_params=pltpu.CompilerParams(
            collective_id=0, has_side_effects=True, vmem_limit_bytes=48 * 1024 * 1024
        ),
    )(inputs[0], targets[0].T, w_enc[0].T, b_enc, w_dec[0])
    genc, gdec, gb = outs
    return genc.T[None], gdec[None], gb


def solution(mesh):
    in_specs = (
        P("layer", None, None),
        P("layer", None, "feat"),
        P("layer", None, "feat"),
        P("layer", "feat"),
        P("layer", None, "feat", None),
    )
    out_specs = (P("layer", None, "feat"), P("layer", None, "feat", None), P("layer", "feat"))
    return jax.shard_map(shards, mesh=mesh, in_specs=in_specs, out_specs=out_specs, check_vma=False)
```

```python
import functools

import jax
import jax.numpy as jnp
from jax import lax
from jax.experimental import pallas as pl
from jax.experimental.pallas import tpu as pltpu
from jax.sharding import PartitionSpec as P

MESH = pl.DeviceIdType.MESH
F32 = jnp.float32
BF16 = jnp.bfloat16

NX = 4
NZ = 8
NT = (((1,), (1,)), ((), ()))


def kernel(
    scale,
    inputs_ref, targets_ref, wenc_ref, benc_ref, wdec_ref,
    genc_ref, gdec_ref, gb_ref,
    x_in, w_en, b_en, t_in, w_all, act_t, a_mat, pre_s, part, y_out, y_in,
    zp_out, zm_out, zp_in, zm_in, x_out, x_sum, x_rec, err, grads, zeros, acc, acc_in, ge_out, gb_out,
    load_sem, zero_sem, store_sem, fin_sem,
    w_s, w_r, t_s, t_r, bb_s, bb_r, a_s, a_r, c_s, c_r, g_s, g_r,
    y_s, y_r, zp_s, zp_r, zm_s, zm_r, x_s, x_r, e_s, e_r, ed_s, ep_s, ep_r, em_s, em_r, b_s, b_r,
):
    lay = lax.axis_index("layer")
    ft = lax.axis_index("feat")
    y_lo = lay // NX
    x = lay % NX
    z = ft // 4
    y_hi = (ft // 2) % 2
    c = ft % 2
    half = w_all.shape[2]
    slab = wdec_ref.shape[1]

    def feat_of(zz, hh):
        return zz * 4 + hh * 2 + c

    partner = (lay, ft + 1 - 2 * c)
    def way(j):
        return 1 - 2 * (j % 2)

    def z_up(j):
        return (z + NZ + way(j)) % NZ

    def z_dn(j):
        return (z + NZ - way(j)) % NZ

    other_lay = (1 - y_lo) * NX + x
    my_cols = pl.ds(pl.multiple_of(c * half, 128), half)
    their_cols = pl.ds(pl.multiple_of((1 - c) * half, 128), half)

    def remote(src, dst, s, r, dev):
        return pltpu.make_async_remote_copy(
            src_ref=src, dst_ref=dst, send_sem=s, recv_sem=r, device_id=dev, device_id_type=MESH
        )

    ld_w = [
        pltpu.make_async_copy(wenc_ref, w_en.at[pl.ds(0, slab), :], load_sem.at[0]),
        pltpu.make_async_copy(inputs_ref, x_in, load_sem.at[1]),
        pltpu.make_async_copy(benc_ref, b_en.at[0], load_sem.at[2]),
        pltpu.make_async_copy(targets_ref, t_in.at[0], load_sem.at[3]),
    ]
    for d in ld_w:
        d.start()

    def own_w(m):
        return pltpu.make_async_copy(
            wdec_ref.at[m, :, my_cols], w_all.at[m, pl.ds(0, slab), :], load_sem.at[4 + m]
        )

    def in_order(start):
        def body(m, _):
            start(m)
            return 0

        lax.fori_loop(jnp.maximum(lay, NX), 2 * NX, body, 0)
        lax.fori_loop(lay, NX, body, 0)

    in_order(lambda m: own_w(m).start())

    barrier = pltpu.get_barrier_semaphore()

    def greet(dev):
        pl.semaphore_signal(barrier, inc=1, device_id=dev, device_id_type=MESH)

    greet(partner)
    greet((lay, feat_of(z_up(0), y_hi)))
    greet((lay, feat_of(z_dn(0), y_hi)))
    greet((other_lay, feat_of(z, y_hi)))
    greet((other_lay, feat_of(z, 1 - y_hi)))
    for k in range(1, NX):
        mate = y_lo * NX + (x + k) % NX
        greet((mate, feat_of(z, y_hi)))
        greet((mate, feat_of(z, 1 - y_hi)))
        greet((mate, feat_of((z + 1) % NZ, y_hi)))
        greet((mate, feat_of((z + NZ - 1) % NZ, y_hi)))
    greet((lay, feat_of(z, 1 - y_hi)))
    zeros[...] = jnp.zeros_like(zeros)
    pl.semaphore_wait(barrier, 18)

    def swap_w(m):
        return remote(
            wdec_ref.at[m, :, their_cols], w_all.at[m, pl.ds(slab, slab), :], w_s.at[m], w_r.at[m], partner
        )

    swap_e = remote(wenc_ref, w_en.at[pl.ds(slab, slab), :], a_s, a_r, partner)
    swap_e.start()
    swap_b = remote(benc_ref, b_en.at[1], bb_s, bb_r, partner)
    swap_b.start()
    swap_t = remote(targets_ref, t_in.at[1], t_s, t_r, partner)
    swap_t.start()

    in_order(lambda m: swap_w(m).start())

    def zero_copy(m):
        return pltpu.make_async_copy(zeros, gdec_ref.at[m], zero_sem.at[m])

    def zero_body(m, _):
        zero_copy(m).start()
        return 0

    lax.fori_loop(0, lay, zero_body, 0)

    row = lax.broadcasted_iota(jnp.int32, (slab, slab), 0)
    col = lax.broadcasted_iota(jnp.int32, (slab, slab), 1)
    ld_w[2].wait()
    swap_b.wait_recv()
    bias = jnp.concatenate(
        [jnp.sum(jnp.where(row == col, b_en[i], 0.0), axis=1, keepdims=True) for i in range(2)], axis=0
    )
    ld_w[0].wait()
    ld_w[1].wait()
    swap_e.wait_recv()
    pre = lax.dot_general(w_en[...], x_in[...], NT, preferred_element_type=F32) + bias
    pre_s[...] = pre[:slab]
    act = jnp.maximum(pre, 0.0).astype(BF16)
    act_t[...] = act
    a_mat[...] = act.T
    ld_w[3].wait()
    swap_t.wait_recv()

    chunk = 384

    def wait_w(m):
        own_w(m).wait()
        swap_w(m).wait_recv()

    def y_copy(j, tb):
        dev = (other_lay, feat_of(z, (y_hi + tb) % 2))
        return remote(y_out.at[j, tb], y_in.at[j, tb], y_s.at[j, tb], y_r.at[j, tb], dev)

    order = (4, -3, 3, -2, 2, -1, 1, 0)

    @pl.when(y_lo == 0)
    def _():
        def up_body(j, _):
            m = NX + j
            wait_w(m)
            for n in range(0, half, chunk):
                p = jnp.dot(a_mat[...], w_all[m, :, pl.ds(n, chunk)], preferred_element_type=F32)
                y_out[j, :, :, pl.ds(n, chunk)] = p.astype(BF16).reshape(NZ, 16, chunk)
            for off in order[:2]:
                y_copy(j, (z + NZ + way(j) * off) % NZ).start()
            return 0

        lax.fori_loop(0, NX, up_body, 0)
        for off in order[2:]:

            def send_body(j, _):
                y_copy(j, (z + NZ + way(j) * off) % NZ).start()
                return 0

            lax.fori_loop(0, NX, send_body, 0)

    lo = jnp.where(y_lo == 1, 0, x)

    def row_part(j):
        m = y_lo * NX + j

        @pl.when(m >= lay)
        def _():
            wait_w(m)
            for n in range(0, half, chunk):
                p = jnp.dot(a_mat[...], w_all[m, :, pl.ds(n, chunk)], preferred_element_type=F32)
                part[j, :, :, pl.ds(n, chunk)] = p.reshape(NZ, 16, chunk)

        @pl.when(m < lay)
        def _():
            part[j] = jnp.zeros(part.shape[1:], F32)

        @pl.when((z // 4 == c) & (j == x))
        def _():
            width = t_in.shape[1]
            for k in range(2):
                core = c if k == 0 else 1 - c
                start = width * (2 * ((2 * z + y_hi) % NZ) + core)
                tt = t_in[k].astype(F32).T.astype(BF16)
                for n in range(0, half, chunk):
                    jj = lax.broadcasted_iota(jnp.int32, (width, chunk), 0) + start
                    nn = lax.broadcasted_iota(jnp.int32, (width, chunk), 1) + n
                    sel = jnp.where(jj == nn, -1.0, 0.0).astype(BF16)
                    t_full = jnp.dot(tt, sel, preferred_element_type=F32)
                    part[x, :, :, pl.ds(n, chunk)] = part[x, :, :, pl.ds(n, chunk)] + t_full.reshape(
                        NZ, 16, chunk
                    )

    def absorb(j, tb):
        @pl.when(y_lo == 1)
        def _():
            y_copy(j, tb).wait_recv()
            part[j, tb] = part[j, tb] + y_in[j, tb].astype(F32)

    def rs_up(s, j):
        return remote(zp_out.at[s, j], zp_in.at[s, j], zp_s.at[s, j], zp_r.at[s, j], (lay, feat_of(z_up(j), y_hi)))

    def rs_dn(s, j):
        return remote(zm_out.at[s, j], zm_in.at[s, j], zm_s.at[s, j], zm_r.at[s, j], (lay, feat_of(z_dn(j), y_hi)))

    for s in range(4):

        def rs_body(j, _):
            t_up = (z + NZ + way(j) * (4 - s)) % NZ
            t_dn = (z + NZ - way(j) * (3 - s)) % NZ
            if s == 0:
                row_part(j)
            absorb(j, t_up)
            v = part[j, t_up]
            if s > 0:
                rs_up(s - 1, j).wait_recv()
                v = v + zp_in[s - 1, j].astype(F32)
            zp_out[s, j] = v.astype(BF16)
            rs_up(s, j).start()
            if s < 3:
                absorb(j, t_dn)
                w = part[j, t_dn]
                if s > 0:
                    rs_dn(s - 1, j).wait_recv()
                    w = w + zm_in[s - 1, j].astype(F32)
                zm_out[s, j] = w.astype(BF16)
                rs_dn(s, j).start()
            return 0

        lax.fori_loop(lo, NX, rs_body, 0)

    def x_same(j):
        return remote(
            x_out.at[j], x_rec.at[x], x_s.at[j], x_r.at[x], (y_lo * NX + j, feat_of(z, y_hi))
        )

    def x_twin(j):
        return remote(
            x_out.at[j], x_rec.at[NX + x], x_s.at[NX + j], x_r.at[NX + x], (y_lo * NX + j, feat_of(z, 1 - y_hi))
        )

    def x_wait(slot):
        remote(x_out.at[0], x_rec.at[slot], x_s.at[0], x_r.at[slot], partner).wait_recv()

    def x_body(j, _):
        absorb(j, z)
        rs_dn(2, j).wait_recv()
        rs_up(3, j).wait_recv()
        v = part[j, z] + zm_in[2, j].astype(F32) + zp_in[3, j].astype(F32)
        x_out[j] = v.astype(BF16)
        x_twin(j).start()

        @pl.when(j != x)
        def _():
            x_same(j).start()

        @pl.when(j == x)
        def _():
            x_sum[...] = v

        return 0

    lax.fori_loop(lo, NX, x_body, 0)

    n_src = jnp.where(y_lo == 1, NX, x + 1)

    def sum_body(xx, _):
        @pl.when(xx != x)
        def _():
            x_wait(xx)
            x_sum[...] = x_sum[...] + x_rec[xx].astype(F32)

        x_wait(NX + xx)
        x_sum[...] = x_sum[...] + x_rec[NX + xx].astype(F32)
        return 0

    lax.fori_loop(0, n_src, sum_body, 0)
    err[lay, z] = x_sum[...].astype(BF16)

    def e_send(xx):
        return remote(
            err.at[lay, z], err.at[lay, z], e_s.at[xx], e_r.at[x], (y_lo * NX + xx, feat_of(z, y_hi))
        )

    def e_wait(j):
        remote(err.at[lay, z], err.at[y_lo * NX + j, z], e_s.at[0], e_r.at[j], partner).wait_recv()

    n_dst = jnp.where(y_lo == 1, NX, x)

    def ag_up(s, j, tb):
        piece = err.at[y_lo * NX + j, tb]
        return remote(piece, piece, ep_s.at[s, j], ep_r.at[s, j], (lay, feat_of(z_up(j), y_hi)))

    def ag_dn(s, j, tb):
        piece = err.at[y_lo * NX + j, tb]
        return remote(piece, piece, em_s.at[s, j], em_r.at[s, j], (lay, feat_of(z_dn(j), y_hi)))

    def back(j, tb):
        piece = err.at[NX + j, tb]
        return remote(
            piece, piece, b_s.at[j, tb], b_r.at[j, tb], (other_lay, feat_of(z, (y_hi + tb + j) % 2))
        )

    def forward_back(j, tb):
        @pl.when(y_lo == 1)
        def _():
            back(j, tb).start()

    def e_up(xx):
        return remote(
            err.at[lay, z], err.at[lay, z], ed_s.at[0, xx], ep_r.at[0, x], (y_lo * NX + xx, feat_of(z_up(x), y_hi))
        )

    def e_dn(xx):
        return remote(
            err.at[lay, z], err.at[lay, z], ed_s.at[1, xx], em_r.at[0, x], (y_lo * NX + xx, feat_of(z_dn(x), y_hi))
        )

    ag_up(0, x, z).start()
    ag_dn(0, x, z).start()

    def e_body(xx, _):
        @pl.when(xx != x)
        def _():
            @pl.when((xx + x) % 2 == 1)
            def _():
                e_up(xx).start()
                e_dn(xx).start()

            e_send(xx).start()

        return 0

    lax.fori_loop(0, n_dst, e_body, 0)
    forward_back(x, z)

    def gdec_own(m):
        return pltpu.make_async_copy(
            grads.at[m, pl.ds(0, slab), :], gdec_ref.at[m, :, my_cols], store_sem.at[m]
        )

    def gdec_peer(m):
        return remote(
            grads.at[m, pl.ds(slab, slab), :], gdec_ref.at[m, :, my_cols], g_s.at[m], g_r.at[m], partner
        )

    def gdec_wait(m):
        remote(
            grads.at[m, pl.ds(slab, slab), :], gdec_ref.at[m, :, their_cols], g_s.at[m], g_r.at[m], partner
        ).wait_recv()

    acc[...] = jnp.zeros_like(acc)

    def decoder_grad(m):
        for n in range(0, half, chunk):
            e = err[m, :, :, pl.ds(n, chunk)].reshape(NZ * 16, chunk)
            g = jnp.dot(act_t[...], e, preferred_element_type=F32) * scale
            grads[m, :, pl.ds(n, chunk)] = g.astype(BF16)
        gdec_peer(m).start()
        gdec_own(m).start()

    def backward(m):
        e = err[m].reshape(NZ * 16, half)
        acc[...] = acc[...] + lax.dot_general(w_all[m], e, NT, preferred_element_type=F32)

        @pl.when(m < 2 * NX - 1)
        def _():
            decoder_grad(m)

    for s in range(5):

        def ag_body(j, _):
            t_up = (z + NZ - way(j) * s) % NZ
            t_dn = (z + NZ + way(j) * s) % NZ
            if s == 0:

                @pl.when(j != x)
                def _():
                    e_wait(j)

                    @pl.when((j + x) % 2 == 0)
                    def _():
                        ag_up(0, j, z).start()
                        ag_dn(0, j, z).start()

                    forward_back(j, z)

            else:
                ag_up(s - 1, j, t_up).wait_recv()
                if s < 4:
                    ag_up(s, j, t_up).start()
                forward_back(j, t_up)
                if s < 4:
                    ag_dn(s - 1, j, t_dn).wait_recv()
                    if s < 3:
                        ag_dn(s, j, t_dn).start()
                    forward_back(j, t_dn)
            return 0

        lax.fori_loop(lo, NX, ag_body, 0)

    def row_back(j, _):
        backward(y_lo * NX + j)
        return 0

    lax.fori_loop(x, NX, row_back, 0)

    @pl.when(y_lo == 0)
    def _():
        def up_back(j, _):
            def wait_body(tb, _):
                back(j, tb).wait_recv()
                return 0

            lax.fori_loop(0, NZ, wait_body, 0)
            backward(NX + j)
            return 0

        lax.fori_loop(0, NX, up_back, 0)

    swap_c = remote(acc.at[pl.ds(slab, slab), :], acc_in, c_s, c_r, partner)
    swap_c.start()
    decoder_grad(2 * NX - 1)
    swap_c.wait_recv()
    act_grad = (acc[pl.ds(0, slab), :] + acc_in[...]) * scale
    pre_grad = jnp.where(pre_s[...] > 0.0, act_grad, 0.0).astype(BF16)
    ge_out[...] = jnp.dot(pre_grad, x_in[...], preferred_element_type=F32).astype(BF16)
    total = jnp.sum(pre_grad.astype(F32), axis=1, keepdims=True)
    gb_out[...] = jnp.sum(jnp.where(row == col, total, 0.0), axis=0, keepdims=True)
    st_e = pltpu.make_async_copy(ge_out, genc_ref, fin_sem.at[0])
    st_b = pltpu.make_async_copy(gb_out, gb_ref, fin_sem.at[1])
    st_e.start()
    st_b.start()

    swap_t.wait_send()
    swap_e.wait_send()
    swap_b.wait_send()
    swap_c.wait_send()

    def own_done(m, _):
        swap_w(m).wait_send()
        gdec_own(m).wait()
        gdec_peer(m).wait_send()
        gdec_wait(m)
        return 0

    lax.fori_loop(lay, 8, own_done, 0)

    def zero_done(m, _):
        zero_copy(m).wait()
        return 0

    lax.fori_loop(0, lay, zero_done, 0)

    def chain_done(j, _):
        @pl.when((j + x) % 2 == 0)
        def _():
            ag_up(0, j, z).wait_send()
            ag_dn(0, j, z).wait_send()

        for s in range(4):
            rs_up(s, j).wait_send()
            if s > 0:
                ag_up(s, j, z).wait_send()
        for s in range(3):
            rs_dn(s, j).wait_send()
            if s > 0:
                ag_dn(s, j, z).wait_send()
        x_twin(j).wait_send()

        @pl.when(j != x)
        def _():
            x_same(j).wait_send()

        return 0

    lax.fori_loop(lo, NX, chain_done, 0)

    def e_done(xx, _):
        @pl.when(xx != x)
        def _():
            e_send(xx).wait_send()

            @pl.when((xx + x) % 2 == 1)
            def _():
                e_up(xx).wait_send()
                e_dn(xx).wait_send()

        return 0

    lax.fori_loop(0, n_dst, e_done, 0)

    def y_done(i, _):
        @pl.when(y_lo == 0)
        def _():
            y_copy(i // NZ, i % NZ).wait_send()

        @pl.when(y_lo == 1)
        def _():
            back(i // NZ, i % NZ).wait_send()

        return 0

    lax.fori_loop(0, NX * NZ, y_done, 0)
    st_e.wait()
    st_b.wait()


def copy_out(a_ref, b_ref, c_ref, a_out, b_out, c_out, sem):
    pairs = ((b_ref, b_out), (a_ref, a_out), (c_ref, c_out))
    copies = [pltpu.make_async_copy(src, dst, sem.at[i]) for i, (src, dst) in enumerate(pairs)]
    for d in copies:
        d.start()
    for d in copies:
        d.wait()


def shards(inputs, targets, w_enc, b_enc, w_dec):
    tok, width = inputs.shape[1], inputs.shape[2]
    n_lay, slab = w_dec.shape[1], w_dec.shape[2]
    half = width // 2
    tcols = targets.shape[2]
    dma = pltpu.SemaphoreType.DMA
    vm = pltpu.VMEM
    any_spec = pl.BlockSpec(memory_space=pl.ANY)
    piece = (16, half)
    outs = pl.pallas_call(
        functools.partial(kernel, tok ** (-0.5)),
        out_shape=(
            jax.ShapeDtypeStruct((slab, width), BF16),
            jax.ShapeDtypeStruct((n_lay, slab, width), BF16),
            jax.ShapeDtypeStruct((1, slab), F32),
        ),
        in_specs=[pl.BlockSpec(memory_space=pltpu.HBM)] * 5,
        out_specs=(any_spec,) * 3,
        scratch_shapes=[
            vm((tok, width), BF16),
            vm((2 * slab, width), BF16),
            vm((2, 1, slab), F32),
            vm((2, tcols, tok), BF16),
            vm((n_lay, 2 * slab, half), BF16),
            vm((2 * slab, tok), BF16),
            vm((tok, 2 * slab), BF16),
            vm((slab, tok), F32),
            vm((NX, NZ) + piece, F32),
            vm((NX, NZ) + piece, BF16),
            vm((NX, NZ) + piece, BF16),
            vm((4, NX) + piece, BF16),
            vm((3, NX) + piece, BF16),
            vm((4, NX) + piece, BF16),
            vm((3, NX) + piece, BF16),
            vm((NX,) + piece, BF16),
            vm(piece, F32),
            vm((2 * NX,) + piece, BF16),
            vm((n_lay, NZ) + piece, BF16),
            vm((n_lay, 2 * slab, half), BF16),
            vm((slab, width), BF16),
            vm((2 * slab, tok), F32),
            vm((slab, tok), F32),
            vm((slab, width), BF16),
            vm((1, slab), F32),
            dma((4 + n_lay,)),
            dma((n_lay,)),
            dma((n_lay,)),
            dma((2,)),
            dma((n_lay,)), dma((n_lay,)),
            dma, dma,
            dma, dma,
            dma, dma,
            dma, dma,
            dma((n_lay,)), dma((n_lay,)),
            dma((NX, NZ)), dma((NX, NZ)),
            dma((4, NX)), dma((4, NX)),
            dma((3, NX)), dma((3, NX)),
            dma((2 * NX,)), dma((2 * NX,)),
            dma((NX,)), dma((NX,)), dma((2, NX)),
            dma((4, NX)), dma((4, NX)),
            dma((3, NX)), dma((3, NX)),
            dma((NX, NZ)), dma((NX, NZ)),
        ],
        compiler_params=pltpu.CompilerParams(
            collective_id=0, has_side_effects=True, vmem_limit_bytes=48 * 1024 * 1024
        ),
    )(*(pltpu.with_memory_space_constraint(a, pltpu.HBM) for a in (inputs[0], targets[0].T, w_enc[0].T, b_enc, w_dec[0])))
    genc, gdec, gb = pl.pallas_call(
        copy_out,
        out_shape=tuple(jax.ShapeDtypeStruct(o.shape, o.dtype) for o in outs),
        in_specs=[any_spec] * 3,
        out_specs=(pl.BlockSpec(memory_space=pltpu.HBM),) * 3,
        scratch_shapes=[dma((3,))],
        compiler_params=pltpu.CompilerParams(vmem_limit_bytes=1024 * 1024),
    )(*outs)
    return genc.T[None], gdec[None], gb


def solution(mesh):
    in_specs = (
        P("layer", None, None),
        P("layer", None, "feat"),
        P("layer", None, "feat"),
        P("layer", "feat"),
        P("layer", None, "feat", None),
    )
    out_specs = (P("layer", None, "feat"), P("layer", None, "feat", None), P("layer", "feat"))
    return jax.shard_map(shards, mesh=mesh, in_specs=in_specs, out_specs=out_specs, check_vma=False)
```

```python
import functools

import jax
import jax.numpy as jnp
from jax import lax
from jax.experimental import pallas as pl
from jax.experimental.pallas import tpu as pltpu
from jax.sharding import PartitionSpec as P

MESH = pl.DeviceIdType.MESH
F32 = jnp.float32
BF16 = jnp.bfloat16

NX = 4
NZ = 8
NT = (((1,), (1,)), ((), ()))


def kernel(
    scale,
    inputs_ref, targets_ref, wenc_ref, benc_ref, wdec_ref,
    genc_ref, gdec_ref, gb_ref,
    x_in, w_en, b_en, t_in, w_all, act_t, a_mat, pre_s, part, y_out, y_in,
    zp_out, zm_out, zp_in, zm_in, x_out, x_sum, x_rec, err, grads, zeros, acc, acc_in, ge_out, gb_out,
    load_sem, zero_sem, store_sem, fin_sem,
    w_s, w_r, t_s, t_r, bb_s, bb_r, a_s, a_r, c_s, c_r, g_s, g_r,
    y_s, y_r, zp_s, zp_r, zm_s, zm_r, x_s, x_r, e_s, e_r, ed_s, ep_s, ep_r, em_s, em_r, b_s, b_r,
):
    lay = lax.axis_index("layer")
    ft = lax.axis_index("feat")
    y_lo = lay // NX
    x = lay % NX
    z = ft // 4
    y_hi = (ft // 2) % 2
    c = ft % 2
    half = w_all.shape[2]
    slab = wdec_ref.shape[1]

    def feat_of(zz, hh):
        return zz * 4 + hh * 2 + c

    partner = (lay, ft + 1 - 2 * c)
    def way(j):
        return 1 - 2 * (j % 2)

    def z_up(j):
        return (z + NZ + way(j)) % NZ

    def z_dn(j):
        return (z + NZ - way(j)) % NZ

    other_lay = (1 - y_lo) * NX + x
    my_cols = pl.ds(pl.multiple_of(c * half, 128), half)
    their_cols = pl.ds(pl.multiple_of((1 - c) * half, 128), half)

    def remote(src, dst, s, r, dev):
        return pltpu.make_async_remote_copy(
            src_ref=src, dst_ref=dst, send_sem=s, recv_sem=r, device_id=dev, device_id_type=MESH
        )

    ld_w = [
        pltpu.make_async_copy(wenc_ref, w_en.at[pl.ds(0, slab), :], load_sem.at[0]),
        pltpu.make_async_copy(inputs_ref, x_in, load_sem.at[1]),
        pltpu.make_async_copy(benc_ref, b_en.at[0], load_sem.at[2]),
        pltpu.make_async_copy(targets_ref, t_in.at[0], load_sem.at[3]),
    ]
    for d in ld_w:
        d.start()

    def own_w(m):
        return pltpu.make_async_copy(
            wdec_ref.at[m, :, my_cols], w_all.at[m, pl.ds(0, slab), :], load_sem.at[4 + m]
        )

    def in_order(start):
        def body(m, _):
            start(m)
            return 0

        lax.fori_loop(jnp.maximum(lay, NX), 2 * NX, body, 0)
        lax.fori_loop(lay, NX, body, 0)

    in_order(lambda m: own_w(m).start())

    barrier = pltpu.get_barrier_semaphore()

    def greet(dev):
        pl.semaphore_signal(barrier, inc=1, device_id=dev, device_id_type=MESH)

    greet(partner)
    greet((lay, feat_of(z_up(0), y_hi)))
    greet((lay, feat_of(z_dn(0), y_hi)))
    greet((other_lay, feat_of(z, y_hi)))
    greet((other_lay, feat_of(z, 1 - y_hi)))
    for k in range(1, NX):
        mate = y_lo * NX + (x + k) % NX
        greet((mate, feat_of(z, y_hi)))
        greet((mate, feat_of(z, 1 - y_hi)))
        greet((mate, feat_of((z + 1) % NZ, y_hi)))
        greet((mate, feat_of((z + NZ - 1) % NZ, y_hi)))
    greet((lay, feat_of(z, 1 - y_hi)))
    zeros[...] = jnp.zeros_like(zeros)
    pl.semaphore_wait(barrier, 18)

    def swap_w(m):
        return remote(
            wdec_ref.at[m, :, their_cols], w_all.at[m, pl.ds(slab, slab), :], w_s.at[m], w_r.at[m], partner
        )

    swap_e = remote(wenc_ref, w_en.at[pl.ds(slab, slab), :], a_s, a_r, partner)
    swap_e.start()
    swap_b = remote(benc_ref, b_en.at[1], bb_s, bb_r, partner)
    swap_b.start()
    swap_t = remote(targets_ref, t_in.at[1], t_s, t_r, partner)
    swap_t.start()

    in_order(lambda m: swap_w(m).start())

    def zero_copy(m):
        return pltpu.make_async_copy(zeros, gdec_ref.at[m], zero_sem.at[m])

    def zero_body(m, _):
        zero_copy(m).start()
        return 0

    lax.fori_loop(0, lay, zero_body, 0)

    row = lax.broadcasted_iota(jnp.int32, (slab, slab), 0)
    col = lax.broadcasted_iota(jnp.int32, (slab, slab), 1)
    ld_w[2].wait()
    swap_b.wait_recv()
    bias = jnp.concatenate(
        [jnp.sum(jnp.where(row == col, b_en[i], 0.0), axis=1, keepdims=True) for i in range(2)], axis=0
    )
    ld_w[0].wait()
    ld_w[1].wait()
    swap_e.wait_recv()
    pre = lax.dot_general(w_en[...], x_in[...], NT, preferred_element_type=F32) + bias
    pre_s[...] = pre[:slab]
    act = jnp.maximum(pre, 0.0).astype(BF16)
    act_t[...] = act
    a_mat[...] = act.T
    ld_w[3].wait()
    swap_t.wait_recv()

    chunk = 384

    def wait_w(m):
        own_w(m).wait()
        swap_w(m).wait_recv()

    def y_copy(j, tb):
        dev = (other_lay, feat_of(z, (y_hi + tb) % 2))
        return remote(y_out.at[j, tb], y_in.at[j, tb], y_s.at[j, tb], y_r.at[j, tb], dev)

    order = (4, -3, 3, -2, 2, -1, 1, 0)

    @pl.when(y_lo == 0)
    def _():
        def up_body(j, _):
            m = NX + j
            wait_w(m)
            for n in range(0, half, chunk):
                p = jnp.dot(a_mat[...], w_all[m, :, pl.ds(n, chunk)], preferred_element_type=F32)
                y_out[j, :, :, pl.ds(n, chunk)] = p.astype(BF16).reshape(NZ, 16, chunk)
            for off in order[:2]:
                y_copy(j, (z + NZ + way(j) * off) % NZ).start()
            return 0

        lax.fori_loop(0, NX, up_body, 0)

    def send_rest():
        for off in order[2:]:

            def send_body(j, _):
                y_copy(j, (z + NZ + way(j) * off) % NZ).start()
                return 0

            lax.fori_loop(0, NX, send_body, 0)

    lo = jnp.where(y_lo == 1, 0, x)

    def row_part(j):
        m = y_lo * NX + j

        @pl.when(m >= lay)
        def _():
            wait_w(m)
            for n in range(0, half, chunk):
                p = jnp.dot(a_mat[...], w_all[m, :, pl.ds(n, chunk)], preferred_element_type=F32)
                part[j, :, :, pl.ds(n, chunk)] = p.reshape(NZ, 16, chunk)

        @pl.when(m < lay)
        def _():
            part[j] = jnp.zeros(part.shape[1:], F32)

        @pl.when((z // 4 == c) & (j == x))
        def _():
            width = t_in.shape[1]
            for k in range(2):
                core = c if k == 0 else 1 - c
                start = width * (2 * ((2 * z + y_hi) % NZ) + core)
                tt = t_in[k].astype(F32).T.astype(BF16)
                for n in range(0, half, chunk):
                    jj = lax.broadcasted_iota(jnp.int32, (width, chunk), 0) + start
                    nn = lax.broadcasted_iota(jnp.int32, (width, chunk), 1) + n
                    sel = jnp.where(jj == nn, -1.0, 0.0).astype(BF16)
                    t_full = jnp.dot(tt, sel, preferred_element_type=F32)
                    part[x, :, :, pl.ds(n, chunk)] = part[x, :, :, pl.ds(n, chunk)] + t_full.reshape(
                        NZ, 16, chunk
                    )

    def absorb(j, tb):
        @pl.when(y_lo == 1)
        def _():
            y_copy(j, tb).wait_recv()
            part[j, tb] = part[j, tb] + y_in[j, tb].astype(F32)

    def rs_up(s, j):
        return remote(zp_out.at[s, j], zp_in.at[s, j], zp_s.at[s, j], zp_r.at[s, j], (lay, feat_of(z_up(j), y_hi)))

    def rs_dn(s, j):
        return remote(zm_out.at[s, j], zm_in.at[s, j], zm_s.at[s, j], zm_r.at[s, j], (lay, feat_of(z_dn(j), y_hi)))

    for s in range(4):

        def rs_body(j, _):
            t_up = (z + NZ + way(j) * (4 - s)) % NZ
            t_dn = (z + NZ - way(j) * (3 - s)) % NZ
            if s == 0:
                row_part(j)
            absorb(j, t_up)
            v = part[j, t_up]
            if s > 0:
                rs_up(s - 1, j).wait_recv()
                v = v + zp_in[s - 1, j].astype(F32)
            zp_out[s, j] = v.astype(BF16)
            rs_up(s, j).start()
            if s < 3:
                absorb(j, t_dn)
                w = part[j, t_dn]
                if s > 0:
                    rs_dn(s - 1, j).wait_recv()
                    w = w + zm_in[s - 1, j].astype(F32)
                zm_out[s, j] = w.astype(BF16)
                rs_dn(s, j).start()
            return 0

        lax.fori_loop(lo, NX, rs_body, 0)
        if s == 0:
            pl.when(y_lo == 0)(send_rest)

    def x_same(j):
        return remote(
            x_out.at[j], x_rec.at[x], x_s.at[j], x_r.at[x], (y_lo * NX + j, feat_of(z, y_hi))
        )

    def x_twin(j):
        return remote(
            x_out.at[j], x_rec.at[NX + x], x_s.at[NX + j], x_r.at[NX + x], (y_lo * NX + j, feat_of(z, 1 - y_hi))
        )

    def x_wait(slot):
        remote(x_out.at[0], x_rec.at[slot], x_s.at[0], x_r.at[slot], partner).wait_recv()

    def x_body(j, _):
        absorb(j, z)
        rs_dn(2, j).wait_recv()
        rs_up(3, j).wait_recv()
        v = part[j, z] + zm_in[2, j].astype(F32) + zp_in[3, j].astype(F32)
        x_out[j] = v.astype(BF16)
        x_twin(j).start()

        @pl.when(j != x)
        def _():
            x_same(j).start()

        @pl.when(j == x)
        def _():
            x_sum[...] = v

        return 0

    lax.fori_loop(lo, NX, x_body, 0)

    n_src = jnp.where(y_lo == 1, NX, x + 1)

    def sum_body(xx, _):
        @pl.when(xx != x)
        def _():
            x_wait(xx)
            x_sum[...] = x_sum[...] + x_rec[xx].astype(F32)

        x_wait(NX + xx)
        x_sum[...] = x_sum[...] + x_rec[NX + xx].astype(F32)
        return 0

    lax.fori_loop(0, n_src, sum_body, 0)
    err[lay, z] = x_sum[...].astype(BF16)

    def e_send(xx):
        return remote(
            err.at[lay, z], err.at[lay, z], e_s.at[xx], e_r.at[x], (y_lo * NX + xx, feat_of(z, y_hi))
        )

    def e_wait(j):
        remote(err.at[lay, z], err.at[y_lo * NX + j, z], e_s.at[0], e_r.at[j], partner).wait_recv()

    n_dst = jnp.where(y_lo == 1, NX, x)

    def ag_up(s, j, tb):
        piece = err.at[y_lo * NX + j, tb]
        return remote(piece, piece, ep_s.at[s, j], ep_r.at[s, j], (lay, feat_of(z_up(j), y_hi)))

    def ag_dn(s, j, tb):
        piece = err.at[y_lo * NX + j, tb]
        return remote(piece, piece, em_s.at[s, j], em_r.at[s, j], (lay, feat_of(z_dn(j), y_hi)))

    def back(j, tb):
        piece = err.at[NX + j, tb]
        return remote(
            piece, piece, b_s.at[j, tb], b_r.at[j, tb], (other_lay, feat_of(z, (y_hi + tb + j) % 2))
        )

    def forward_back(j, tb):
        @pl.when(y_lo == 1)
        def _():
            back(j, tb).start()

    def e_up(xx):
        return remote(
            err.at[lay, z], err.at[lay, z], ed_s.at[0, xx], ep_r.at[0, x], (y_lo * NX + xx, feat_of(z_up(x), y_hi))
        )

    def e_dn(xx):
        return remote(
            err.at[lay, z], err.at[lay, z], ed_s.at[1, xx], em_r.at[0, x], (y_lo * NX + xx, feat_of(z_dn(x), y_hi))
        )

    ag_up(0, x, z).start()
    ag_dn(0, x, z).start()

    def e_body(xx, _):
        @pl.when(xx != x)
        def _():
            e_send(xx).start()

            @pl.when((xx + x) % 2 == 1)
            def _():
                e_up(xx).start()
                e_dn(xx).start()


        return 0

    lax.fori_loop(0, n_dst, e_body, 0)
    forward_back(x, z)

    def gdec_own(m):
        return pltpu.make_async_copy(
            grads.at[m, pl.ds(0, slab), :], gdec_ref.at[m, :, my_cols], store_sem.at[m]
        )

    def gdec_peer(m):
        return remote(
            grads.at[m, pl.ds(slab, slab), :], gdec_ref.at[m, :, my_cols], g_s.at[m], g_r.at[m], partner
        )

    def gdec_wait(m):
        remote(
            grads.at[m, pl.ds(slab, slab), :], gdec_ref.at[m, :, their_cols], g_s.at[m], g_r.at[m], partner
        ).wait_recv()

    acc[...] = jnp.zeros_like(acc)

    def decoder_grad(m):
        for n in range(0, half, chunk):
            e = err[m, :, :, pl.ds(n, chunk)].reshape(NZ * 16, chunk)
            g = jnp.dot(act_t[...], e, preferred_element_type=F32) * scale
            grads[m, :, pl.ds(n, chunk)] = g.astype(BF16)
        gdec_peer(m).start()
        gdec_own(m).start()

    def backward(m):
        e = err[m].reshape(NZ * 16, half)
        acc[...] = acc[...] + lax.dot_general(w_all[m], e, NT, preferred_element_type=F32)

        @pl.when(m < 2 * NX - 1)
        def _():
            decoder_grad(m)

    for s in range(5):

        def ag_body(j, _):
            t_up = (z + NZ - way(j) * s) % NZ
            t_dn = (z + NZ + way(j) * s) % NZ
            if s == 0:

                @pl.when(j != x)
                def _():
                    e_wait(j)

                    @pl.when((j + x) % 2 == 0)
                    def _():
                        ag_up(0, j, z).start()
                        ag_dn(0, j, z).start()

                    forward_back(j, z)

            else:
                ag_up(s - 1, j, t_up).wait_recv()
                if s < 4:
                    ag_up(s, j, t_up).start()
                forward_back(j, t_up)
                if s < 4:
                    ag_dn(s - 1, j, t_dn).wait_recv()
                    if s < 3:
                        ag_dn(s, j, t_dn).start()
                    forward_back(j, t_dn)
            return 0

        lax.fori_loop(lo, NX, ag_body, 0)

    def row_back(j, _):
        backward(y_lo * NX + j)
        return 0

    lax.fori_loop(x, NX, row_back, 0)

    @pl.when(y_lo == 0)
    def _():
        def up_back(j, _):
            def wait_body(tb, _):
                back(j, tb).wait_recv()
                return 0

            lax.fori_loop(0, NZ, wait_body, 0)
            backward(NX + j)
            return 0

        lax.fori_loop(0, NX, up_back, 0)

    swap_c = remote(acc.at[pl.ds(slab, slab), :], acc_in, c_s, c_r, partner)
    swap_c.start()
    decoder_grad(2 * NX - 1)
    swap_c.wait_recv()
    act_grad = (acc[pl.ds(0, slab), :] + acc_in[...]) * scale
    pre_grad = jnp.where(pre_s[...] > 0.0, act_grad, 0.0).astype(BF16)
    ge_out[...] = jnp.dot(pre_grad, x_in[...], preferred_element_type=F32).astype(BF16)
    total = jnp.sum(pre_grad.astype(F32), axis=1, keepdims=True)
    gb_out[...] = jnp.sum(jnp.where(row == col, total, 0.0), axis=0, keepdims=True)
    st_e = pltpu.make_async_copy(ge_out, genc_ref, fin_sem.at[0])
    st_b = pltpu.make_async_copy(gb_out, gb_ref, fin_sem.at[1])
    st_e.start()
    st_b.start()

    swap_t.wait_send()
    swap_e.wait_send()
    swap_b.wait_send()
    swap_c.wait_send()

    def own_done(m, _):
        swap_w(m).wait_send()
        gdec_own(m).wait()
        gdec_peer(m).wait_send()
        gdec_wait(m)
        return 0

    lax.fori_loop(lay, 8, own_done, 0)

    def zero_done(m, _):
        zero_copy(m).wait()
        return 0

    lax.fori_loop(0, lay, zero_done, 0)

    def chain_done(j, _):
        @pl.when((j + x) % 2 == 0)
        def _():
            ag_up(0, j, z).wait_send()
            ag_dn(0, j, z).wait_send()

        for s in range(4):
            rs_up(s, j).wait_send()
            if s > 0:
                ag_up(s, j, z).wait_send()
        for s in range(3):
            rs_dn(s, j).wait_send()
            if s > 0:
                ag_dn(s, j, z).wait_send()
        x_twin(j).wait_send()

        @pl.when(j != x)
        def _():
            x_same(j).wait_send()

        return 0

    lax.fori_loop(lo, NX, chain_done, 0)

    def e_done(xx, _):
        @pl.when(xx != x)
        def _():
            e_send(xx).wait_send()

            @pl.when((xx + x) % 2 == 1)
            def _():
                e_up(xx).wait_send()
                e_dn(xx).wait_send()

        return 0

    lax.fori_loop(0, n_dst, e_done, 0)

    def y_done(i, _):
        @pl.when(y_lo == 0)
        def _():
            y_copy(i // NZ, i % NZ).wait_send()

        @pl.when(y_lo == 1)
        def _():
            back(i // NZ, i % NZ).wait_send()

        return 0

    lax.fori_loop(0, NX * NZ, y_done, 0)
    st_e.wait()
    st_b.wait()


def copy_out(a_ref, b_ref, c_ref, a_out, b_out, c_out, sem):
    pairs = ((b_ref, b_out), (a_ref, a_out), (c_ref, c_out))
    copies = [pltpu.make_async_copy(src, dst, sem.at[i]) for i, (src, dst) in enumerate(pairs)]
    for d in copies:
        d.start()
    for d in copies:
        d.wait()


def shards(inputs, targets, w_enc, b_enc, w_dec):
    tok, width = inputs.shape[1], inputs.shape[2]
    n_lay, slab = w_dec.shape[1], w_dec.shape[2]
    half = width // 2
    tcols = targets.shape[2]
    dma = pltpu.SemaphoreType.DMA
    vm = pltpu.VMEM
    any_spec = pl.BlockSpec(memory_space=pl.ANY)
    piece = (16, half)
    outs = pl.pallas_call(
        functools.partial(kernel, tok ** (-0.5)),
        out_shape=(
            jax.ShapeDtypeStruct((slab, width), BF16),
            jax.ShapeDtypeStruct((n_lay, slab, width), BF16),
            jax.ShapeDtypeStruct((1, slab), F32),
        ),
        in_specs=[pl.BlockSpec(memory_space=pltpu.HBM)] * 5,
        out_specs=(any_spec,) * 3,
        scratch_shapes=[
            vm((tok, width), BF16),
            vm((2 * slab, width), BF16),
            vm((2, 1, slab), F32),
            vm((2, tcols, tok), BF16),
            vm((n_lay, 2 * slab, half), BF16),
            vm((2 * slab, tok), BF16),
            vm((tok, 2 * slab), BF16),
            vm((slab, tok), F32),
            vm((NX, NZ) + piece, F32),
            vm((NX, NZ) + piece, BF16),
            vm((NX, NZ) + piece, BF16),
            vm((4, NX) + piece, BF16),
            vm((3, NX) + piece, BF16),
            vm((4, NX) + piece, BF16),
            vm((3, NX) + piece, BF16),
            vm((NX,) + piece, BF16),
            vm(piece, F32),
            vm((2 * NX,) + piece, BF16),
            vm((n_lay, NZ) + piece, BF16),
            vm((n_lay, 2 * slab, half), BF16),
            vm((slab, width), BF16),
            vm((2 * slab, tok), F32),
            vm((slab, tok), F32),
            vm((slab, width), BF16),
            vm((1, slab), F32),
            dma((4 + n_lay,)),
            dma((n_lay,)),
            dma((n_lay,)),
            dma((2,)),
            dma((n_lay,)), dma((n_lay,)),
            dma, dma,
            dma, dma,
            dma, dma,
            dma, dma,
            dma((n_lay,)), dma((n_lay,)),
            dma((NX, NZ)), dma((NX, NZ)),
            dma((4, NX)), dma((4, NX)),
            dma((3, NX)), dma((3, NX)),
            dma((2 * NX,)), dma((2 * NX,)),
            dma((NX,)), dma((NX,)), dma((2, NX)),
            dma((4, NX)), dma((4, NX)),
            dma((3, NX)), dma((3, NX)),
            dma((NX, NZ)), dma((NX, NZ)),
        ],
        compiler_params=pltpu.CompilerParams(
            collective_id=0, has_side_effects=True, vmem_limit_bytes=48 * 1024 * 1024
        ),
    )(*(pltpu.with_memory_space_constraint(a, pltpu.HBM) for a in (inputs[0], targets[0].T, w_enc[0].T, b_enc, w_dec[0])))
    genc, gdec, gb = pl.pallas_call(
        copy_out,
        out_shape=tuple(jax.ShapeDtypeStruct(o.shape, o.dtype) for o in outs),
        in_specs=[any_spec] * 3,
        out_specs=(pl.BlockSpec(memory_space=pltpu.HBM),) * 3,
        scratch_shapes=[dma((3,))],
        compiler_params=pltpu.CompilerParams(vmem_limit_bytes=1024 * 1024),
    )(*outs)
    return genc.T[None], gdec[None], gb


def solution(mesh):
    in_specs = (
        P("layer", None, None),
        P("layer", None, "feat"),
        P("layer", None, "feat"),
        P("layer", "feat"),
        P("layer", None, "feat", None),
    )
    out_specs = (P("layer", None, "feat"), P("layer", None, "feat", None), P("layer", "feat"))
    return jax.shard_map(shards, mesh=mesh, in_specs=in_specs, out_specs=out_specs, check_vma=False)
```

```python
import functools

import jax
import jax.numpy as jnp
from jax import lax
from jax.experimental import pallas as pl
from jax.experimental.pallas import tpu as pltpu
from jax.sharding import PartitionSpec as P

MESH = pl.DeviceIdType.MESH
F32 = jnp.float32
BF16 = jnp.bfloat16

NX = 4
NZ = 8
NT = (((1,), (1,)), ((), ()))


def kernel(
    scale,
    inputs_ref, targets_ref, wenc_ref, benc_ref, wdec_ref,
    genc_ref, gdec_ref, gb_ref,
    x_in, w_en, b_en, t_in, w_all, act_t, a_mat, pre_s, part, y_out, y_in,
    zp_out, zm_out, zp_in, zm_in, x_out, x_sum, x_rec, err, grads, zeros, acc, acc_in, ge_out, gb_out,
    load_sem, zero_sem, store_sem, fin_sem,
    w_s, w_r, t_s, t_r, bb_s, bb_r, a_s, a_r, c_s, c_r, g_s, g_r,
    y_s, y_r, zp_s, zp_r, zm_s, zm_r, x_s, x_r, e_s, e_r, ed_s, ep_s, ep_r, em_s, em_r, b_s, b_r,
):
    lay = lax.axis_index("layer")
    ft = lax.axis_index("feat")
    y_lo = lay // NX
    x = lay % NX
    z = ft // 4
    y_hi = (ft // 2) % 2
    c = ft % 2
    half = w_all.shape[2]
    slab = wdec_ref.shape[1]

    def feat_of(zz, hh):
        return zz * 4 + hh * 2 + c

    partner = (lay, ft + 1 - 2 * c)
    def way(j):
        return 1 - 2 * (j % 2)

    def z_up(j):
        return (z + NZ + way(j)) % NZ

    def z_dn(j):
        return (z + NZ - way(j)) % NZ

    other_lay = (1 - y_lo) * NX + x
    my_cols = pl.ds(pl.multiple_of(c * half, 128), half)
    their_cols = pl.ds(pl.multiple_of((1 - c) * half, 128), half)

    def remote(src, dst, s, r, dev):
        return pltpu.make_async_remote_copy(
            src_ref=src, dst_ref=dst, send_sem=s, recv_sem=r, device_id=dev, device_id_type=MESH
        )

    ld_w = [
        pltpu.make_async_copy(wenc_ref, w_en.at[pl.ds(0, slab), :], load_sem.at[0]),
        pltpu.make_async_copy(inputs_ref, x_in, load_sem.at[1]),
        pltpu.make_async_copy(benc_ref, b_en.at[0], load_sem.at[2]),
        pltpu.make_async_copy(targets_ref, t_in.at[0], load_sem.at[3]),
    ]
    for d in ld_w:
        d.start()

    def own_w(m):
        return pltpu.make_async_copy(
            wdec_ref.at[m, :, my_cols], w_all.at[m, pl.ds(0, slab), :], load_sem.at[4 + m]
        )

    def in_order(start):
        def body(m, _):
            start(m)
            return 0

        lax.fori_loop(jnp.maximum(lay, NX), 2 * NX, body, 0)
        lax.fori_loop(lay, NX, body, 0)

    in_order(lambda m: own_w(m).start())

    barrier = pltpu.get_barrier_semaphore()

    def greet(dev):
        pl.semaphore_signal(barrier, inc=1, device_id=dev, device_id_type=MESH)

    greet(partner)
    greet((lay, feat_of(z_up(0), y_hi)))
    greet((lay, feat_of(z_dn(0), y_hi)))
    greet((other_lay, feat_of(z, y_hi)))
    greet((other_lay, feat_of(z, 1 - y_hi)))
    for k in range(1, NX):
        mate = y_lo * NX + (x + k) % NX
        greet((mate, feat_of(z, y_hi)))
        greet((mate, feat_of(z, 1 - y_hi)))
        if k % 2 == 1:
            greet((mate, feat_of((z + 1) % NZ, y_hi)))
            greet((mate, feat_of((z + NZ - 1) % NZ, y_hi)))
    greet((lay, feat_of(z, 1 - y_hi)))
    zeros[...] = jnp.zeros_like(zeros)
    pl.semaphore_wait(barrier, 16)

    def swap_w(m):
        return remote(
            wdec_ref.at[m, :, their_cols], w_all.at[m, pl.ds(slab, slab), :], w_s.at[m], w_r.at[m], partner
        )

    swap_e = remote(wenc_ref, w_en.at[pl.ds(slab, slab), :], a_s, a_r, partner)
    swap_e.start()
    swap_b = remote(benc_ref, b_en.at[1], bb_s, bb_r, partner)
    swap_b.start()
    swap_t = remote(targets_ref, t_in.at[1], t_s, t_r, partner)
    swap_t.start()

    in_order(lambda m: swap_w(m).start())

    def zero_copy(m):
        return pltpu.make_async_copy(zeros, gdec_ref.at[m], zero_sem.at[m])

    def zero_body(m, _):
        zero_copy(m).start()
        return 0

    lax.fori_loop(0, lay, zero_body, 0)

    row = lax.broadcasted_iota(jnp.int32, (slab, slab), 0)
    col = lax.broadcasted_iota(jnp.int32, (slab, slab), 1)
    ld_w[2].wait()
    swap_b.wait_recv()
    bias = jnp.concatenate(
        [jnp.sum(jnp.where(row == col, b_en[i], 0.0), axis=1, keepdims=True) for i in range(2)], axis=0
    )
    ld_w[0].wait()
    ld_w[1].wait()
    swap_e.wait_recv()
    pre = lax.dot_general(w_en[...], x_in[...], NT, preferred_element_type=F32) + bias
    pre_s[...] = pre[:slab]
    act = jnp.maximum(pre, 0.0).astype(BF16)
    act_t[...] = act
    a_mat[...] = act.T
    ld_w[3].wait()
    swap_t.wait_recv()

    chunk = half

    def wait_w(m):
        own_w(m).wait()
        swap_w(m).wait_recv()

    def y_copy(j, tb):
        dev = (other_lay, feat_of(z, (y_hi + tb) % 2))
        return remote(y_out.at[j, tb], y_in.at[j, tb], y_s.at[j, tb], y_r.at[j, tb], dev)

    order = (4, -3, 3, -2, 2, -1, 1, 0)

    @pl.when(y_lo == 0)
    def _():
        def up_body(j, _):
            m = NX + j
            wait_w(m)
            for n in range(0, half, chunk):
                p = jnp.dot(a_mat[...], w_all[m, :, pl.ds(n, chunk)], preferred_element_type=F32)
                y_out[j, :, :, pl.ds(n, chunk)] = p.astype(BF16).reshape(NZ, 16, chunk)
            for off in order[:2]:
                y_copy(j, (z + NZ + way(j) * off) % NZ).start()
            return 0

        lax.fori_loop(0, NX, up_body, 0)

    def send_rest():
        for off in order[2:]:

            def send_body(j, _):
                y_copy(j, (z + NZ + way(j) * off) % NZ).start()
                return 0

            lax.fori_loop(0, NX, send_body, 0)

    lo = jnp.where(y_lo == 1, 0, x)

    def row_part(j):
        m = y_lo * NX + j

        @pl.when(m >= lay)
        def _():
            wait_w(m)
            for n in range(0, half, chunk):
                p = jnp.dot(a_mat[...], w_all[m, :, pl.ds(n, chunk)], preferred_element_type=F32)
                part[j, :, :, pl.ds(n, chunk)] = p.reshape(NZ, 16, chunk)

        @pl.when(m < lay)
        def _():
            part[j] = jnp.zeros(part.shape[1:], F32)

        @pl.when((z // 4 == c) & (j == x))
        def _():
            width = t_in.shape[1]
            for k in range(2):
                core = c if k == 0 else 1 - c
                start = width * (2 * ((2 * z + y_hi) % NZ) + core)
                tt = t_in[k].astype(F32).T.astype(BF16)
                for n in range(0, half, chunk):
                    jj = lax.broadcasted_iota(jnp.int32, (width, chunk), 0) + start
                    nn = lax.broadcasted_iota(jnp.int32, (width, chunk), 1) + n
                    sel = jnp.where(jj == nn, -1.0, 0.0).astype(BF16)
                    t_full = jnp.dot(tt, sel, preferred_element_type=F32)
                    part[x, :, :, pl.ds(n, chunk)] = part[x, :, :, pl.ds(n, chunk)] + t_full.reshape(
                        NZ, 16, chunk
                    )

    def absorb(j, tb):
        @pl.when(y_lo == 1)
        def _():
            y_copy(j, tb).wait_recv()
            part[j, tb] = part[j, tb] + y_in[j, tb].astype(F32)

    def rs_up(s, j):
        return remote(zp_out.at[s, j], zp_in.at[s, j], zp_s.at[s, j], zp_r.at[s, j], (lay, feat_of(z_up(j), y_hi)))

    def rs_dn(s, j):
        return remote(zm_out.at[s, j], zm_in.at[s, j], zm_s.at[s, j], zm_r.at[s, j], (lay, feat_of(z_dn(j), y_hi)))

    for s in range(4):

        def rs_body(j, _):
            t_up = (z + NZ + way(j) * (4 - s)) % NZ
            t_dn = (z + NZ - way(j) * (3 - s)) % NZ
            if s == 0:
                row_part(j)
            absorb(j, t_up)
            v = part[j, t_up]
            if s > 0:
                rs_up(s - 1, j).wait_recv()
                v = v + zp_in[s - 1, j].astype(F32)
            zp_out[s, j] = v.astype(BF16)
            rs_up(s, j).start()
            if s < 3:
                absorb(j, t_dn)
                w = part[j, t_dn]
                if s > 0:
                    rs_dn(s - 1, j).wait_recv()
                    w = w + zm_in[s - 1, j].astype(F32)
                zm_out[s, j] = w.astype(BF16)
                rs_dn(s, j).start()
            return 0

        lax.fori_loop(lo, NX, rs_body, 0)
        if s == 0:
            pl.when(y_lo == 0)(send_rest)

    def x_same(j):
        return remote(
            x_out.at[j], x_rec.at[x], x_s.at[j], x_r.at[x], (y_lo * NX + j, feat_of(z, y_hi))
        )

    def x_twin(j):
        return remote(
            x_out.at[j], x_rec.at[NX + x], x_s.at[NX + j], x_r.at[NX + x], (y_lo * NX + j, feat_of(z, 1 - y_hi))
        )

    def x_wait(slot):
        remote(x_out.at[0], x_rec.at[slot], x_s.at[0], x_r.at[slot], partner).wait_recv()

    def x_body(j, _):
        absorb(j, z)
        rs_dn(2, j).wait_recv()
        rs_up(3, j).wait_recv()
        v = part[j, z] + zm_in[2, j].astype(F32) + zp_in[3, j].astype(F32)
        x_out[j] = v.astype(BF16)
        x_twin(j).start()

        @pl.when(j != x)
        def _():
            x_same(j).start()

        @pl.when(j == x)
        def _():
            x_sum[...] = v

        return 0

    lax.fori_loop(lo, NX, x_body, 0)

    n_src = jnp.where(y_lo == 1, NX, x + 1)

    def sum_body(xx, _):
        @pl.when(xx != x)
        def _():
            x_wait(xx)
            x_sum[...] = x_sum[...] + x_rec[xx].astype(F32)

        x_wait(NX + xx)
        x_sum[...] = x_sum[...] + x_rec[NX + xx].astype(F32)
        return 0

    lax.fori_loop(0, n_src, sum_body, 0)
    err[lay, z] = x_sum[...].astype(BF16)

    def e_send(xx):
        return remote(
            err.at[lay, z], err.at[lay, z], e_s.at[xx], e_r.at[x], (y_lo * NX + xx, feat_of(z, y_hi))
        )

    def e_wait(j):
        remote(err.at[lay, z], err.at[y_lo * NX + j, z], e_s.at[0], e_r.at[j], partner).wait_recv()

    n_dst = jnp.where(y_lo == 1, NX, x)

    def ag_up(s, j, tb):
        piece = err.at[y_lo * NX + j, tb]
        return remote(piece, piece, ep_s.at[s, j], ep_r.at[s, j], (lay, feat_of(z_up(j), y_hi)))

    def ag_dn(s, j, tb):
        piece = err.at[y_lo * NX + j, tb]
        return remote(piece, piece, em_s.at[s, j], em_r.at[s, j], (lay, feat_of(z_dn(j), y_hi)))

    def back(j, tb):
        piece = err.at[NX + j, tb]
        return remote(
            piece, piece, b_s.at[j, tb], b_r.at[j, tb], (other_lay, feat_of(z, (y_hi + tb + j) % 2))
        )

    def forward_back(j, tb):
        @pl.when(y_lo == 1)
        def _():
            back(j, tb).start()

    def e_up(xx):
        return remote(
            err.at[lay, z], err.at[lay, z], ed_s.at[0, xx], ep_r.at[0, x], (y_lo * NX + xx, feat_of(z_up(x), y_hi))
        )

    def e_dn(xx):
        return remote(
            err.at[lay, z], err.at[lay, z], ed_s.at[1, xx], em_r.at[0, x], (y_lo * NX + xx, feat_of(z_dn(x), y_hi))
        )

    ag_up(0, x, z).start()
    ag_dn(0, x, z).start()

    def e_body(xx, _):
        @pl.when(xx != x)
        def _():
            e_send(xx).start()

            @pl.when((xx + x) % 2 == 1)
            def _():
                e_up(xx).start()
                e_dn(xx).start()


        return 0

    lax.fori_loop(0, n_dst, e_body, 0)
    forward_back(x, z)

    def gdec_own(m):
        return pltpu.make_async_copy(
            grads.at[m, pl.ds(0, slab), :], gdec_ref.at[m, :, my_cols], store_sem.at[m]
        )

    def gdec_peer(m):
        return remote(
            grads.at[m, pl.ds(slab, slab), :], gdec_ref.at[m, :, my_cols], g_s.at[m], g_r.at[m], partner
        )

    def gdec_wait(m):
        remote(
            grads.at[m, pl.ds(slab, slab), :], gdec_ref.at[m, :, their_cols], g_s.at[m], g_r.at[m], partner
        ).wait_recv()

    acc[...] = jnp.zeros_like(acc)

    def decoder_grad(m):
        for n in range(0, half, chunk):
            e = err[m, :, :, pl.ds(n, chunk)].reshape(NZ * 16, chunk)
            g = jnp.dot(act_t[...], e, preferred_element_type=F32) * scale
            grads[m, :, pl.ds(n, chunk)] = g.astype(BF16)
        gdec_peer(m).start()
        gdec_own(m).start()

    def backward(m):
        e = err[m].reshape(NZ * 16, half)
        acc[...] = acc[...] + lax.dot_general(w_all[m], e, NT, preferred_element_type=F32)

        @pl.when(m < 2 * NX - 1)
        def _():
            decoder_grad(m)

    for s in range(5):

        def ag_body(j, _):
            t_up = (z + NZ - way(j) * s) % NZ
            t_dn = (z + NZ + way(j) * s) % NZ
            if s == 0:

                @pl.when(j != x)
                def _():
                    e_wait(j)

                    @pl.when((j + x) % 2 == 0)
                    def _():
                        ag_up(0, j, z).start()
                        ag_dn(0, j, z).start()

                    forward_back(j, z)

            else:
                ag_up(s - 1, j, t_up).wait_recv()
                if s < 4:
                    ag_up(s, j, t_up).start()
                forward_back(j, t_up)
                if s < 4:
                    ag_dn(s - 1, j, t_dn).wait_recv()
                    if s < 3:
                        ag_dn(s, j, t_dn).start()
                    forward_back(j, t_dn)
            return 0

        lax.fori_loop(lo, NX, ag_body, 0)

    def row_back(j, _):
        backward(y_lo * NX + j)
        return 0

    lax.fori_loop(x, NX, row_back, 0)

    @pl.when(y_lo == 0)
    def _():
        def up_back(j, _):
            def wait_body(tb, _):
                back(j, tb).wait_recv()
                return 0

            lax.fori_loop(0, NZ, wait_body, 0)
            backward(NX + j)
            return 0

        lax.fori_loop(0, NX, up_back, 0)

    swap_c = remote(acc.at[pl.ds(slab, slab), :], acc_in, c_s, c_r, partner)
    swap_c.start()
    decoder_grad(2 * NX - 1)
    swap_c.wait_recv()
    act_grad = (acc[pl.ds(0, slab), :] + acc_in[...]) * scale
    pre_grad = jnp.where(pre_s[...] > 0.0, act_grad, 0.0).astype(BF16)
    ge_out[...] = jnp.dot(pre_grad, x_in[...], preferred_element_type=F32).astype(BF16)
    total = jnp.sum(pre_grad.astype(F32), axis=1, keepdims=True)
    gb_out[...] = jnp.sum(jnp.where(row == col, total, 0.0), axis=0, keepdims=True)
    st_e = pltpu.make_async_copy(ge_out, genc_ref, fin_sem.at[0])
    st_b = pltpu.make_async_copy(gb_out, gb_ref, fin_sem.at[1])
    st_e.start()
    st_b.start()

    swap_t.wait_send()
    swap_e.wait_send()
    swap_b.wait_send()
    swap_c.wait_send()

    def own_done(m, _):
        swap_w(m).wait_send()
        gdec_own(m).wait()
        gdec_peer(m).wait_send()
        gdec_wait(m)
        return 0

    lax.fori_loop(lay, 8, own_done, 0)

    def zero_done(m, _):
        zero_copy(m).wait()
        return 0

    lax.fori_loop(0, lay, zero_done, 0)

    def chain_done(j, _):
        @pl.when((j + x) % 2 == 0)
        def _():
            ag_up(0, j, z).wait_send()
            ag_dn(0, j, z).wait_send()

        for s in range(4):
            rs_up(s, j).wait_send()
            if s > 0:
                ag_up(s, j, z).wait_send()
        for s in range(3):
            rs_dn(s, j).wait_send()
            if s > 0:
                ag_dn(s, j, z).wait_send()
        x_twin(j).wait_send()

        @pl.when(j != x)
        def _():
            x_same(j).wait_send()

        return 0

    lax.fori_loop(lo, NX, chain_done, 0)

    def e_done(xx, _):
        @pl.when(xx != x)
        def _():
            e_send(xx).wait_send()

            @pl.when((xx + x) % 2 == 1)
            def _():
                e_up(xx).wait_send()
                e_dn(xx).wait_send()

        return 0

    lax.fori_loop(0, n_dst, e_done, 0)

    def y_done(i, _):
        @pl.when(y_lo == 0)
        def _():
            y_copy(i // NZ, i % NZ).wait_send()

        @pl.when(y_lo == 1)
        def _():
            back(i // NZ, i % NZ).wait_send()

        return 0

    lax.fori_loop(0, NX * NZ, y_done, 0)
    st_e.wait()
    st_b.wait()


def copy_out(a_ref, b_ref, c_ref, a_out, b_out, c_out, sem):
    pairs = ((b_ref, b_out), (a_ref, a_out), (c_ref, c_out))
    copies = [pltpu.make_async_copy(src, dst, sem.at[i]) for i, (src, dst) in enumerate(pairs)]
    for d in copies:
        d.start()
    for d in copies:
        d.wait()


def shards(inputs, targets, w_enc, b_enc, w_dec):
    tok, width = inputs.shape[1], inputs.shape[2]
    n_lay, slab = w_dec.shape[1], w_dec.shape[2]
    half = width // 2
    tcols = targets.shape[2]
    dma = pltpu.SemaphoreType.DMA
    vm = pltpu.VMEM
    any_spec = pl.BlockSpec(memory_space=pl.ANY)
    piece = (16, half)
    outs = pl.pallas_call(
        functools.partial(kernel, tok ** (-0.5)),
        out_shape=(
            jax.ShapeDtypeStruct((slab, width), BF16),
            jax.ShapeDtypeStruct((n_lay, slab, width), BF16),
            jax.ShapeDtypeStruct((1, slab), F32),
        ),
        in_specs=[pl.BlockSpec(memory_space=pltpu.HBM)] * 5,
        out_specs=(any_spec,) * 3,
        scratch_shapes=[
            vm((tok, width), BF16),
            vm((2 * slab, width), BF16),
            vm((2, 1, slab), F32),
            vm((2, tcols, tok), BF16),
            vm((n_lay, 2 * slab, half), BF16),
            vm((2 * slab, tok), BF16),
            vm((tok, 2 * slab), BF16),
            vm((slab, tok), F32),
            vm((NX, NZ) + piece, F32),
            vm((NX, NZ) + piece, BF16),
            vm((NX, NZ) + piece, BF16),
            vm((4, NX) + piece, BF16),
            vm((3, NX) + piece, BF16),
            vm((4, NX) + piece, BF16),
            vm((3, NX) + piece, BF16),
            vm((NX,) + piece, BF16),
            vm(piece, F32),
            vm((2 * NX,) + piece, BF16),
            vm((n_lay, NZ) + piece, BF16),
            vm((n_lay, 2 * slab, half), BF16),
            vm((slab, width), BF16),
            vm((2 * slab, tok), F32),
            vm((slab, tok), F32),
            vm((slab, width), BF16),
            vm((1, slab), F32),
            dma((4 + n_lay,)),
            dma((n_lay,)),
            dma((n_lay,)),
            dma((2,)),
            dma((n_lay,)), dma((n_lay,)),
            dma, dma,
            dma, dma,
            dma, dma,
            dma, dma,
            dma((n_lay,)), dma((n_lay,)),
            dma((NX, NZ)), dma((NX, NZ)),
            dma((4, NX)), dma((4, NX)),
            dma((3, NX)), dma((3, NX)),
            dma((2 * NX,)), dma((2 * NX,)),
            dma((NX,)), dma((NX,)), dma((2, NX)),
            dma((4, NX)), dma((4, NX)),
            dma((3, NX)), dma((3, NX)),
            dma((NX, NZ)), dma((NX, NZ)),
        ],
        compiler_params=pltpu.CompilerParams(
            collective_id=0, has_side_effects=True, vmem_limit_bytes=48 * 1024 * 1024
        ),
    )(*(pltpu.with_memory_space_constraint(a, pltpu.HBM) for a in (inputs[0], targets[0].T, w_enc[0].T, b_enc, w_dec[0])))
    genc, gdec, gb = pl.pallas_call(
        copy_out,
        out_shape=tuple(jax.ShapeDtypeStruct(o.shape, o.dtype) for o in outs),
        in_specs=[any_spec] * 3,
        out_specs=(pl.BlockSpec(memory_space=pltpu.HBM),) * 3,
        scratch_shapes=[dma((3,))],
        compiler_params=pltpu.CompilerParams(vmem_limit_bytes=1024 * 1024),
    )(*outs)
    return genc.T[None], gdec[None], gb


def solution(mesh):
    in_specs = (
        P("layer", None, None),
        P("layer", None, "feat"),
        P("layer", None, "feat"),
        P("layer", "feat"),
        P("layer", None, "feat", None),
    )
    out_specs = (P("layer", None, "feat"), P("layer", None, "feat", None), P("layer", "feat"))
    return jax.shard_map(shards, mesh=mesh, in_specs=in_specs, out_specs=out_specs, check_vma=False)
```
